256 devices in a mesh: doc: 8 (over z), term: 32 (over y, x, core).
Axes of the slice: x: 4, y: 4, z: 8, core: 2. Of those that a mesh axis runs over, the one named last changes fastest.
Arguments:
- tile_values: bfloat16 [8, 32, 256, 128, 128], P('doc', 'term'), may hold values from -0.03125 to 0.03125
- tile_row: int32 [8, 32, 256], P('doc', 'term'), may hold values from 0 to 31
- tile_col: int32 [8, 32, 256], P('doc', 'term'), may hold values from 0 to 31
- tile_count: int32 [8, 32], P('doc', 'term'), may hold values from 65 to 256, as said below
- targets: float32 [32, 32768], P(None, 'doc'), may hold values from -6 to 6
- ridge_weight: float32 [32], replicated, may hold values from 0.1 to 1
Outputs:
- solution: float32 [32, 131072], P(None, 'term')
- residual: float32 [32, 32768], P(None, 'doc')
- gradient: float32 [32, 131072], P(None, 'term')
The draws below stay inside these ranges and needn't reach their ends.
Inputs may be any that keep to these rules, and one draw needn't show every extreme that they name: `tile_count`: slots at and beyond a device's count are unused; some device has all 256 slots live.
All inputs are finite; a program needn't handle non-finite values.
Results may differ from the reference program's by a relative error of at most 0.023.
Values may be sent and summed in bfloat16 or wider, within the bound.
A program may use at most 64 MiB of HBM per device.

```python
import math
import jax
import jax.numpy as jnp
from jax import lax

TILE = 128
K = 32
RB = 32
CB = 32
SLOTS = 256
ITERS = 2
NDOC = 32768
N_DOC = 8
N_TERM = 32


def draw_tile_count(key, part):
    first_key, second_key = jax.random.split(jax.random.fold_in(key, 11))
    base_counts = jax.random.randint(first_key, (N_DOC * N_TERM,), SLOTS // 4 + 1, SLOTS + 1)
    chosen = jax.random.randint(second_key, (), 0, N_DOC * N_TERM)
    filled = jnp.where(jnp.arange(N_DOC * N_TERM) == chosen, SLOTS, base_counts)
    return filled.reshape(N_DOC, N_TERM).astype(jnp.int32)


def with_ends(drawn, key, smallest, high):
    longest = drawn.shape.index(max(drawn.shape))
    spots = []
    for shift in (0, 1):
        where = [jax.random.randint(jax.random.fold_in(key, axis), (), 0, length) for axis, length in enumerate(drawn.shape)]
        where[longest] = (where[longest] + shift) % drawn.shape[longest]
        spots.append(tuple(where))
    return drawn.at[spots[0]].set(smallest).at[spots[1]].set(high)


def levels(own_key, shape, shards, low, largest):
    def one(axis_at, blocks):
        draws = jax.random.uniform(jax.random.fold_in(jax.random.fold_in(own_key, 6), axis_at), (blocks,), jnp.float32, low / len(shards), largest / len(shards))
        return jnp.repeat(jnp.exp(draws), shape[axis_at] // blocks).reshape((-1,) + (1,) * (len(shape) - axis_at - 1))

    loudness = one(*shards[0])
    for cut in shards[1:]:
        loudness = loudness * one(*cut)
    return loudness


def noise(rng, extent, spread, most, cuts=(), dtype=jnp.bfloat16):
    result = spread * jax.random.normal(rng, extent, jnp.float32)
    if cuts:
        result = result * levels(rng, extent, cuts, -0.22, 0.18)
    return jnp.clip(result, -most, most).astype(dtype)


def setup_inputs(seed: int = 0) -> dict:
    key_list = jax.random.split(jax.random.key(seed), 7)
    return {
        "tile_values": noise(key_list[0], (N_DOC, N_TERM, SLOTS, TILE, TILE), (SLOTS * N_TERM * TILE // RB) ** -0.5, 0.03125, ((0, 8), (1, 32))),
        "tile_row": with_ends(jax.random.randint(key_list[1], (N_DOC, N_TERM, SLOTS), 0, RB), jax.random.fold_in(key_list[1], 1), 0, RB - 1).astype(jnp.int32),
        "tile_col": with_ends(jax.random.randint(key_list[2], (N_DOC, N_TERM, SLOTS), 0, CB), jax.random.fold_in(key_list[2], 1), 0, CB - 1).astype(jnp.int32),
        "tile_count": draw_tile_count(jax.random.fold_in(key_list[6], 71), 0),
        "targets": noise(key_list[4], (K, NDOC), 1.0, 6.0, ((1, 8),), jnp.float32),
        "ridge_weight": jnp.clip(jnp.exp(jax.random.uniform(key_list[5], (K,), jnp.float32, math.log(0.1), math.log(1.0))), 0.1, 1.0),
    }


def forward_tiles(tile_set, row_set, col_set, tile_total, dir_blocks):
    alive_mask = (jnp.arange(tile_set.shape[0]) < tile_total).astype(jnp.float32)
    picked = dir_blocks[:, col_set, :].astype(jnp.float32)
    product = jnp.einsum("sab,ksb->ksa", tile_set.astype(jnp.float32), picked) * alive_mask[None, :, None]
    return jnp.zeros((K, RB, TILE), jnp.float32).at[:, row_set, :].add(product)


def adjoint_tiles(tile_set, row_set, col_set, tile_total, res_blocks):
    alive_mask = (jnp.arange(tile_set.shape[0]) < tile_total).astype(jnp.float32)
    picked = res_blocks[:, row_set, :].astype(jnp.float32)
    product = jnp.einsum("sab,ksa->ksb", tile_set.astype(jnp.float32), picked) * alive_mask[None, :, None]
    return jnp.zeros((K, CB, TILE), jnp.float32).at[:, col_set, :].add(product)


def apply_forward(tile_values, tile_row, tile_col, tile_count, direction):
    dir_blocks = direction.astype(jnp.bfloat16).reshape(K, N_TERM, CB, TILE).transpose(1, 0, 2, 3)

    def per_doc(doc_pos):
        def accumulate(running, inputs):
            tile_set, row_set, col_set, tile_total, blocks_here = inputs
            return running + forward_tiles(tile_set, row_set, col_set, tile_total, blocks_here), None

        running, unused = lax.scan(accumulate, jnp.zeros((K, RB, TILE), jnp.float32),
                                   (tile_values[doc_pos], tile_row[doc_pos], tile_col[doc_pos], tile_count[doc_pos], dir_blocks))
        return running

    stacked = lax.map(per_doc, jnp.arange(N_DOC))
    return stacked.transpose(1, 0, 2, 3).reshape(K, N_DOC * RB * TILE)


def apply_adjoint(tile_values, tile_row, tile_col, tile_count, residual):
    res_blocks = residual.astype(jnp.bfloat16).reshape(K, N_DOC, RB, TILE).transpose(1, 0, 2, 3)

    def per_term(term_pos):
        def accumulate(running, inputs):
            tile_set, row_set, col_set, tile_total, blocks_here = inputs
            return running + adjoint_tiles(tile_set, row_set, col_set, tile_total, blocks_here), None

        running, unused = lax.scan(accumulate, jnp.zeros((K, CB, TILE), jnp.float32),
                                   (tile_values[:, term_pos], tile_row[:, term_pos], tile_col[:, term_pos], tile_count[:, term_pos], res_blocks))
        return running

    stacked = lax.map(per_term, jnp.arange(N_TERM))
    return stacked.transpose(1, 0, 2, 3).reshape(K, N_TERM * CB * TILE)


def reference(tile_values, tile_row, tile_col, tile_count, targets, ridge_weight):
    solution = jnp.zeros((K, N_TERM * CB * TILE), jnp.float32)
    residual = targets
    gradient = apply_adjoint(tile_values, tile_row, tile_col, tile_count, residual)
    direction = gradient
    grad_sq = jnp.sum(gradient * gradient, axis=1)
    for iteration in range(ITERS):
        image_rows = apply_forward(tile_values, tile_row, tile_col, tile_count, direction)
        curvature = jnp.sum(image_rows * image_rows, axis=1) + ridge_weight * jnp.sum(direction * direction, axis=1)
        step_len = grad_sq / curvature
        solution = solution + step_len[:, None] * direction
        residual = residual - step_len[:, None] * image_rows
        gradient = apply_adjoint(tile_values, tile_row, tile_col, tile_count, residual) - ridge_weight[:, None] * solution
        if iteration + 1 < ITERS:
            new_sq = jnp.sum(gradient * gradient, axis=1)
            direction = gradient + (new_sq / grad_sq)[:, None] * direction
            grad_sq = new_sq
    return solution, residual, gradient
```

```python
import functools

import jax
import jax.numpy as jnp
from jax import lax
from jax.experimental import pallas as pl
from jax.experimental.pallas import tpu as pltpu
from jax.sharding import PartitionSpec as P

TILE = 128
K = 32
BLOCKS = 32
SLOTS = 256
UNROLL = 32
F32 = jnp.float32
BF16 = jnp.bfloat16


def slot_tables(tile_row, tile_col, tile_count):
    slot = jnp.arange(SLOTS, dtype=jnp.int32)
    live = slot < tile_count
    dest = jnp.stack([jnp.where(live, tile_col, BLOCKS), jnp.where(live, tile_row, BLOCKS)])
    source = jnp.stack([jnp.where(live, tile_row, BLOCKS), jnp.where(live, tile_col, BLOCKS)])
    order_key = dest * SLOTS + slot[None, :]
    rank = jnp.sum((order_key[:, None, :] < order_key[:, :, None]).astype(jnp.int32), axis=2)
    hit = rank[:, None, :] == slot[None, :, None]
    packed = jnp.sum(jnp.where(hit, ((dest * 64 + source) * SLOTS + slot[None, :])[:, None, :], 0), axis=2)
    perm = packed % SLOTS
    source_sorted = (packed // SLOTS) % 64
    dest_sorted = packed // (SLOTS * 64)
    same = dest_sorted[:, 1:] == dest_sorted[:, :-1]
    keep = jnp.concatenate([jnp.zeros((2, 1), F32), same.astype(F32)], axis=1)
    block = jnp.arange(BLOCKS, dtype=jnp.int32)[None, :, None]
    upto = jnp.sum((dest[:, None, :] <= block).astype(jnp.int32), axis=2)
    here = jnp.sum((dest[:, None, :] == block).astype(jnp.int32), axis=2)
    last = jnp.where(here > 0, upto - 1, SLOTS)
    return perm, source_sorted, keep, last


def sum_lanes(tile, values, base):
    lane = lax.broadcasted_iota(jnp.int32, (8, TILE), 1)
    for group in range(K // 8):
        total = jnp.sum(values[8 * group:8 * group + 8], axis=1, keepdims=True)
        tile = jnp.where(lane == base + group, total, tile)
    return tile


def per_target(tile, base):
    return jnp.concatenate([tile[:, base + g:base + g + 1] for g in range(K // 8)], axis=0)


def cgls_kernel(nd, nt, perm, source, keep, last, targets, ridge_ref, tiles_hbm,
                x_out, r_out, g_out,
                tiles, prod, vr0, vp0, vp1, vg, vq0, vq1,
                send_g, recv_g, send_q, recv_q, q_old, s_held, g_held, p_held, x_held,
                st_doc, st_term,
                tile_sem, gs_sem, gr_sem, qs_sem, qr_sem, pas_sem, par_sem, qas_sem, qar_sem,
                sds_sem, sdr_sem, sts_sem, str_sem):
    me_d = lax.axis_index("doc")
    me_t = lax.axis_index("term")
    gp = BLOCKS // nd
    qp = BLOCKS // nt
    ridge = ridge_ref[...]

    barrier = pltpu.get_barrier_semaphore()

    @pl.loop(1, nd)
    def _(o):
        pl.semaphore_signal(barrier, inc=1, device_id={"doc": lax.rem(me_d + o, nd)})

    @pl.loop(1, nt)
    def _(o):
        pl.semaphore_signal(barrier, inc=1, device_id={"term": lax.rem(me_t + o, nt)})

    load_tiles = pltpu.make_async_copy(tiles_hbm, tiles, tile_sem)
    load_tiles.start()

    zero = jnp.zeros((K, TILE), BF16)
    for v in (vr0, vp0, vp1, vq0, vq1):
        v[BLOCKS] = zero
    prod[SLOTS] = jnp.zeros((K, TILE), F32)
    for b in range(BLOCKS):
        vr0[b] = targets[:, b * TILE:(b + 1) * TILE].astype(BF16)

    def product(which, v, out, middle=None):
        def steps(first, count):
            def body(j, acc):
                for u in range(UNROLL):
                    i = j * UNROLL + u
                    tile = tiles[perm[which, i]]
                    vec = v[source[which, i]]
                    dims = (((1,), (0,)), ((), ())) if which == 0 else (((1,), (1,)), ((), ()))
                    part = lax.dot_general(vec, tile, dims, preferred_element_type=F32)
                    acc = acc * keep[which, i] + part
                    prod[i] = acc
                return acc
            return body

        half = SLOTS // UNROLL // 2
        acc = lax.fori_loop(0, half, steps(0, half), jnp.zeros((K, TILE), F32))
        if middle is not None:
            middle()
        lax.fori_loop(half, 2 * half, steps(half, half), acc)
        for b in range(BLOCKS):
            out[b] = prod[last[which, b]].astype(BF16)

    def wait_bytes(ref, sem):
        pltpu.make_async_copy(ref, ref, sem).wait()

    def scatter_g(n):
        for o in range(1, nd):
            to = lax.rem(me_d + o, nd)
            pltpu.make_async_remote_copy(
                src_ref=send_g.at[n, pl.ds(to * gp, gp)], dst_ref=recv_g.at[n, nd - 1 - o],
                send_sem=gs_sem.at[n], recv_sem=gr_sem.at[n], device_id={"doc": to}).start()

    def summed_g(n, j):
        total = prod[last[0, me_d * gp + j]]
        for s in range(nd - 1):
            total = total + recv_g[n, s, j].astype(F32)
        return total

    def gather_g(n, v):
        for o in range(1, nd):
            to = lax.rem(me_d + o, nd)
            mine = v.at[pl.ds(me_d * gp, gp)]
            pltpu.make_async_remote_copy(
                src_ref=mine, dst_ref=mine, send_sem=pas_sem.at[n], recv_sem=par_sem.at[n],
                device_id={"doc": to}).start()

    def scatter_q(n):
        @pl.loop(1, nt)
        def _(o):
            to = lax.rem(me_t + o, nt)
            pltpu.make_async_remote_copy(
                src_ref=send_q.at[n, pl.ds(to * qp, qp)], dst_ref=recv_q.at[n, nt - 1 - o],
                send_sem=qs_sem.at[n], recv_sem=qr_sem.at[n], device_id={"term": to}).start()

    def summed_q(n, j):
        total = prod[last[1, me_t * qp + j]]
        for s in range(nt - 1):
            total = total + recv_q[n, s, j].astype(F32)
        return total

    def gather_q(n, v):
        @pl.loop(1, nt)
        def _(o):
            to = lax.rem(me_t + o, nt)
            mine = v.at[pl.ds(me_t * qp, qp)]
            pltpu.make_async_remote_copy(
                src_ref=mine, dst_ref=mine, send_sem=qas_sem.at[n], recv_sem=qar_sem.at[n],
                device_id={"term": to}).start()

    def stats_doc_start(n, tile):
        st_doc[n, me_d] = tile
        for o in range(1, nd):
            to = lax.rem(me_d + o, nd)
            mine = st_doc.at[n, me_d]
            pltpu.make_async_remote_copy(
                src_ref=mine, dst_ref=mine, send_sem=sds_sem.at[n], recv_sem=sdr_sem.at[n],
                device_id={"doc": to}).start()

    def stats_doc_sum(n):
        wait_bytes(st_doc.at[n, pl.ds(0, nd - 1)], sdr_sem.at[n])
        total = st_doc[n, 0]
        for s in range(1, nd):
            total = total + st_doc[n, s]
        return total

    def stats_term_start(n, tile):
        st_term[n, me_t] = tile

        @pl.loop(1, nt)
        def _(o):
            to = lax.rem(me_t + o, nt)
            mine = st_term.at[n, me_t]
            pltpu.make_async_remote_copy(
                src_ref=mine, dst_ref=mine, send_sem=sts_sem.at[n], recv_sem=str_sem.at[n],
                device_id={"term": to}).start()

    def stats_term_sum(n):
        wait_bytes(st_term.at[n, pl.ds(0, nt - 1)], str_sem.at[n])
        total = st_term[n, 0]
        for s in range(1, nt):
            total = total + st_term[n, s]
        return total

    empty = jnp.zeros((8, TILE), F32)

    pl.semaphore_wait(barrier, nd + nt - 2)
    load_tiles.wait()

    product(0, vr0, send_g.at[0])
    scatter_g(0)
    wait_bytes(recv_g.at[0], gr_sem.at[0])
    p_sq = jnp.zeros((K, TILE), F32)
    for j in range(gp):
        total = summed_g(0, j)
        s_held[j] = total
        vp0[me_d * gp + j] = total.astype(BF16)
        p_sq = p_sq + total * total
    gather_g(0, vp0)
    wait_bytes(vp0.at[pl.ds(0, (nd - 1) * gp)], par_sem.at[0])

    product(1, vp0, send_q.at[0])
    scatter_q(0)
    wait_bytes(recv_q.at[0], qr_sem.at[0])
    q_sq = jnp.zeros((K, TILE), F32)
    for j in range(qp):
        total = summed_q(0, j)
        q_old[j] = total
        vq0[me_t * qp + j] = total.astype(BF16)
        q_sq = q_sq + total * total
    gather_q(0, vq0)
    stats_doc_start(0, sum_lanes(sum_lanes(empty, p_sq, 0), q_sq + ridge * p_sq, 4))
    wait_bytes(vq0.at[pl.ds(0, (nt - 1) * qp)], qar_sem.at[0])

    product(0, vq0, send_g.at[1], lambda: stats_term_start(0, stats_doc_sum(0)))
    scatter_g(1)
    stats = stats_term_sum(0)
    grad_sq = per_target(stats, 0)
    step0 = grad_sq / per_target(stats, 4)
    wait_bytes(recv_g.at[1], gr_sem.at[1])
    g_sq = jnp.zeros((K, TILE), F32)
    for j in range(gp):
        p = s_held[j]
        s = p - step0 * summed_g(1, j)
        x = step0 * p
        g = s - ridge * x
        p_held[j] = p
        s_held[j] = s
        x_held[j] = x
        g_held[j] = g
        vp1[me_d * gp + j] = g.astype(BF16)
        g_sq = g_sq + g * g
    gather_g(1, vp1)
    stats_term_start(1, sum_lanes(empty, g_sq, 0))
    wait_bytes(vp1.at[pl.ds(0, (nd - 1) * gp)], par_sem.at[1])

    product(1, vp1, send_q.at[1], lambda: stats_doc_start(1, stats_term_sum(1)))
    scatter_q(1)
    new_sq = per_target(stats_doc_sum(1), 0)
    beta = new_sq / grad_sq
    p_sq = jnp.zeros((K, TILE), F32)
    for j in range(gp):
        p = g_held[j] + beta * p_held[j]
        p_held[j] = p
        p_sq = p_sq + p * p
    wait_bytes(recv_q.at[1], qr_sem.at[1])
    q_sq = jnp.zeros((K, TILE), F32)
    for j in range(qp):
        total = summed_q(1, j) + beta * q_old[j]
        vq1[me_t * qp + j] = total.astype(BF16)
        q_sq = q_sq + total * total
    gather_q(1, vq1)
    stats_doc_start(2, sum_lanes(empty, q_sq + ridge * p_sq, 0))
    wait_bytes(vq1.at[pl.ds(0, (nt - 1) * qp)], qar_sem.at[1])

    product(0, vq1, send_g.at[2], lambda: stats_term_start(2, stats_doc_sum(2)))
    scatter_g(2)
    step1 = new_sq / per_target(stats_term_sum(2), 0)
    wait_bytes(recv_g.at[2], gr_sem.at[2])
    for j in range(gp):
        s = s_held[j] - step1 * summed_g(2, j)
        x = x_held[j] + step1 * p_held[j]
        vg[me_d * gp + j] = (s - ridge * x).astype(BF16)
    gather_g(2, vg)
    along0 = step0 + step1 * beta
    for b in range(BLOCKS):
        lanes = slice(b * TILE, (b + 1) * TILE)
        x_out[:, lanes] = along0 * vp0[b].astype(F32) + step1 * vp1[b].astype(F32)
        r_out[:, lanes] = (targets[:, lanes] - step0 * vq0[b].astype(F32)
                           - step1 * vq1[b].astype(F32))
    wait_bytes(vg.at[pl.ds(0, (nd - 1) * gp)], par_sem.at[2])
    for b in range(BLOCKS):
        g_out[:, b * TILE:(b + 1) * TILE] = vg[b].astype(F32)

    for n in range(3):
        wait_bytes(send_g.at[n, pl.ds(0, (nd - 1) * gp)], gs_sem.at[n])
        wait_bytes(vg.at[pl.ds(0, (nd - 1) * gp)], pas_sem.at[n])
        wait_bytes(st_doc.at[n, pl.ds(0, nd - 1)], sds_sem.at[n])
        wait_bytes(st_term.at[n, pl.ds(0, nt - 1)], sts_sem.at[n])
    for n in range(2):
        wait_bytes(send_q.at[n, pl.ds(0, (nt - 1) * qp)], qs_sem.at[n])
        wait_bytes(vq0.at[pl.ds(0, (nt - 1) * qp)], qas_sem.at[n])


def on_device(nd, nt, tile_values, tile_row, tile_col, tile_count, targets, ridge_weight):
    perm, source, keep, last = slot_tables(tile_row[0, 0], tile_col[0, 0], tile_count[0, 0])
    gp = BLOCKS // nd
    qp = BLOCKS // nt
    smem = pl.BlockSpec(memory_space=pltpu.SMEM)
    vmem = pl.BlockSpec(memory_space=pltpu.VMEM)
    dma = pltpu.SemaphoreType.DMA
    out = jax.ShapeDtypeStruct((K, BLOCKS * TILE), F32)
    vector = pltpu.VMEM((BLOCKS + 1, K, TILE), BF16)
    piece = pltpu.VMEM((gp, K, TILE), F32)
    return pl.pallas_call(
        functools.partial(cgls_kernel, nd, nt),
        out_shape=(out, out, out),
        in_specs=[smem, smem, smem, smem, vmem, vmem, pl.BlockSpec(memory_space=pl.ANY)],
        out_specs=(vmem, vmem, vmem),
        scratch_shapes=[
            pltpu.VMEM((SLOTS, TILE, TILE), BF16),
            pltpu.VMEM((SLOTS + 1, K, TILE), F32),
            vector, vector, vector, vector, vector, vector,
            pltpu.VMEM((3, BLOCKS, K, TILE), BF16),
            pltpu.VMEM((3, nd - 1, gp, K, TILE), BF16),
            pltpu.VMEM((2, BLOCKS, K, TILE), BF16),
            pltpu.VMEM((2, nt - 1, qp, K, TILE), BF16),
            pltpu.VMEM((qp, K, TILE), F32),
            piece, piece, piece, piece,
            pltpu.VMEM((3, nd, 8, TILE), F32),
            pltpu.VMEM((3, nt, 8, TILE), F32),
            dma(()), dma((3,)), dma((3,)), dma((2,)), dma((2,)), dma((3,)), dma((3,)), dma((2,)), dma((2,)),
            dma((3,)), dma((3,)), dma((3,)), dma((3,)),
        ],
        compiler_params=pltpu.CompilerParams(
            collective_id=0, has_side_effects=True, vmem_limit_bytes=48 * 1024 * 1024),
        name="cgls",
    )(perm, source, keep, last, targets, ridge_weight.reshape(K, 1), tile_values[0, 0])


def solution(mesh):
    nd, nt = mesh.shape["doc"], mesh.shape["term"]
    placed = (
        P("doc", "term", None, None, None),
        P("doc", "term", None),
        P("doc", "term", None),
        P("doc", "term"),
        P(None, "doc"),
        P(),
    )
    return jax.shard_map(
        functools.partial(on_device, nd, nt),
        mesh=mesh,
        in_specs=placed,
        out_specs=(P(None, "term"), P(None, "doc"), P(None, "term")),
        check_vma=False,
    )
```

```python
import functools

import jax
import jax.numpy as jnp
from jax import lax
from jax.experimental import pallas as pl
from jax.experimental.pallas import tpu as pltpu
from jax.sharding import PartitionSpec as P

TILE = 128
K = 32
BLOCKS = 32
SLOTS = 256
PAIRS = (SLOTS + BLOCKS) // 2
PLACES = 384
UNROLL = 72
LOADS = 8
HALF = K // 2
HALVES = range(2)
F32 = jnp.float32
BF16 = jnp.bfloat16
INT = jnp.int32


def iota(shape, dim):
    return lax.broadcasted_iota(INT, shape, dim)


def upright(row):
    square = (row.shape[1], row.shape[1])
    return jnp.sum(jnp.where(iota(square, 0) == iota(square, 1), row, 0.0), axis=1, keepdims=True)


def slot_tables(row, col, count, table):
    slot = iota((1, SLOTS), 1).astype(F32)
    live = slot < count
    block = iota((SLOTS, TILE), 1).astype(F32)
    place = iota((SLOTS, PLACES), 1).astype(F32)
    before = iota((TILE, TILE), 0) < iota((TILE, TILE), 1)
    for which, (dest, source) in enumerate(((col, row), (row, col))):
        dest = jnp.where(live, dest, float(BLOCKS))
        code = (dest * 64.0 + jnp.where(live, source, float(BLOCKS))) * SLOTS + slot
        code_up = upright(code)
        dest_up = upright(dest)
        here = dest_up == block
        size = jnp.sum(jnp.where(here, 1.0, 0.0), axis=0, keepdims=True).astype(INT)
        padded = jnp.bitwise_and(size + 1, -2)
        start = jnp.sum(jnp.where(before, upright(padded.astype(F32)), 0.0), axis=0, keepdims=True)
        within = jnp.sum(jnp.where(jnp.logical_and(code < code_up, dest == dest_up), 1.0, 0.0),
                         axis=1, keepdims=True)
        position = within + jnp.sum(jnp.where(here, start, 0.0), axis=1, keepdims=True)
        ordered = jnp.sum(jnp.where(position == place, code_up + 1.0, 0.0), axis=0, keepdims=True)
        ordered = ordered.astype(INT) - 1
        filled = ordered >= 0
        ordered = jnp.maximum(ordered, 0)
        dest_at = jnp.right_shift(ordered, 14)
        source_at = jnp.minimum(jnp.bitwise_and(jnp.right_shift(ordered, 8), 63), BLOCKS)
        same = jnp.where(dest_at == pltpu.roll(dest_at, 2, 1), 1, 0)
        last = jnp.right_shift(start.astype(INT) + padded, 1) - 1
        last = jnp.where(size > 0, jnp.clip(last, 0, PAIRS - 1), PAIRS)
        at = 4 * which
        table[at:at + 1, :] = jnp.bitwise_and(ordered, SLOTS - 1)
        table[at + 1:at + 2, :] = jnp.where(filled, source_at, BLOCKS)
        table[at + 2:at + 3, :] = same
        for part in range(PLACES // TILE):
            table[at + 3:at + 4, part * TILE:(part + 1) * TILE] = last


def to_row(values, base):
    total = jnp.sum(values, axis=1, keepdims=True)
    here = iota((HALF, TILE), 1) == iota((HALF, TILE), 0) + base
    return jnp.sum(jnp.where(here, total, 0.0), axis=0, keepdims=True)


def from_row(row, base):
    here = iota((HALF, TILE), 1) == iota((HALF, TILE), 0) + base
    return jnp.sum(jnp.where(here, row, 0.0), axis=1, keepdims=True)


def cgls_kernel(nd, nt, info_hbm, targets_hbm, tiles_hbm,
                x_out, r_out, g_out,
                info, table_v, table, targets,
                tiles, tiles_t, prod, vectors,
                send_g, recv_g, send_q, recv_q, q_old, s_held, g_held, p_held, x_held,
                st_doc, st_term,
                info_sem, table_sem, targets_sem,
                tile_sem, gs_sem, gr_sem, qs_sem, qr_sem, pas_sem, par_sem, qas_sem, qar_sem,
                sds_sem, sdr_sem, sts_sem, str_sem):
    me_d = lax.axis_index("doc")
    me_t = lax.axis_index("term")
    gp = BLOCKS // nd
    vr0, vp0, vp1, vg, vq0, vq1 = (vectors[2 * i:2 * i + 2] for i in range(6))

    barrier = pltpu.get_barrier_semaphore()

    load_info = pltpu.make_async_copy(info_hbm, info, info_sem)
    load_info.start()
    load_targets = pltpu.make_async_copy(targets_hbm, targets, targets_sem)
    load_targets.start()
    part = SLOTS // LOADS
    load_tiles = [
        pltpu.make_async_copy(tiles_hbm.at[pl.ds(i * part, part)], tiles.at[pl.ds(i * part, part)],
                              tile_sem.at[i])
        for i in range(LOADS)
    ]
    for load in load_tiles:
        load.start()

    @pl.loop(1, nd)
    def _(o):
        pl.semaphore_signal(barrier, inc=1, device_id={"doc": lax.rem(me_d + o, nd)})

    @pl.loop(1, nt)
    def _(o):
        pl.semaphore_signal(barrier, inc=1, device_id={"term": lax.rem(me_t + o, nt)})

    zero = jnp.zeros((HALF, TILE), BF16)
    for h in HALVES:
        for v in (vr0, vp0, vp1, vq0, vq1):
            v[h][BLOCKS] = zero
        prod[h, PAIRS] = jnp.zeros((HALF, TILE), F32)

    load_info.wait()
    slot_tables(info[0:1, :], info[1:2, :], info[2:3, :], table_v)
    move_table = pltpu.make_async_copy(table_v, table, table_sem)
    move_table.start()
    ridge_all = upright(info[3:4, :TILE])
    ridge = [ridge_all[h * HALF:(h + 1) * HALF] for h in HALVES]
    load_targets.wait()
    for b in range(BLOCKS):
        for h in HALVES:
            vr0[h][b] = targets[h * HALF:(h + 1) * HALF, b * TILE:(b + 1) * TILE].astype(BF16)
    move_table.wait()
    for load in load_tiles:
        load.wait()

    def product(which, v, h):
        matrix = tiles if which == 0 else tiles_t
        at = 4 * which

        def body(j, acc):
            for u in range(UNROLL):
                i = j * UNROLL + u
                left = jnp.concatenate([v[h][table[at + 1, 2 * i + e]] for e in range(2)], axis=1)
                right = jnp.concatenate([matrix[table[at, 2 * i + e]] for e in range(2)], axis=0)
                acc = (acc * table[at + 2, 2 * i].astype(F32)
                       + jnp.dot(left, right, preferred_element_type=F32))
                prod[h, i] = acc
            return acc

        lax.fori_loop(0, PAIRS // UNROLL, body, jnp.zeros((HALF, TILE), F32))

    def product_block(which, h, b):
        return prod[h, table[4 * which + 3, b]]

    def wait_bytes(ref, sem):
        pltpu.make_async_copy(ref, ref, sem).wait()

    doc_far = sorted(range(1, nd), key=lambda o: -min(o, nd - o))
    ny, nx = nt // 8, 4
    term_far = sorted(
        ((y, x, c) for y in range(ny) for x in range(nx) for c in range(2) if (y, x, c) != (0, 0, 0)),
        key=lambda o: -(min(o[0], ny - o[0]) + min(o[1], nx - o[1])))

    def doc_peer(o):
        return lax.rem(me_d + o, nd)

    def term_peer(o):
        y = lax.rem(me_t // (2 * nx) + o[0], ny)
        x = lax.rem(lax.rem(me_t // 2, nx) + o[1], nx)
        c = lax.rem(me_t + o[2], 2)
        return (y * nx + x) * 2 + c

    def scatter_g(n, h):
        for b in range(BLOCKS):
            send_g[n, h, b] = product_block(0, h, b).astype(BF16)
        for i, o in enumerate(doc_far):
            to = doc_peer(o)
            pltpu.make_async_remote_copy(
                src_ref=send_g.at[n, h, pl.ds(to * gp, gp)], dst_ref=recv_g.at[n, h, i],
                send_sem=gs_sem.at[n, h], recv_sem=gr_sem.at[n, h], device_id={"doc": to}).start()

    def scattered_g(n, h):
        wait_bytes(recv_g.at[n, h], gr_sem.at[n, h])

    def summed_g(n, h, j):
        total = product_block(0, h, me_d * gp + j)
        for s in range(nd - 1):
            total = total + recv_g[n, h, s, j].astype(F32)
        return total

    def gather_g(n, h, v):
        for o in doc_far:
            mine = v[h].at[pl.ds(me_d * gp, gp)]
            pltpu.make_async_remote_copy(
                src_ref=mine, dst_ref=mine, send_sem=pas_sem.at[n, h], recv_sem=par_sem.at[n, h],
                device_id={"doc": doc_peer(o)}).start()

    def gathered_g(n, h, v):
        wait_bytes(v[h].at[pl.ds(0, (nd - 1) * gp)], par_sem.at[n, h])

    def scatter_q(n, h):
        for b in range(BLOCKS):
            send_q[n, h, b] = product_block(1, h, b).astype(BF16)
        for i, o in enumerate(term_far):
            to = term_peer(o)
            pltpu.make_async_remote_copy(
                src_ref=send_q.at[n, h, to], dst_ref=recv_q.at[n, h, i],
                send_sem=qs_sem.at[n, h], recv_sem=qr_sem.at[n, h], device_id={"term": to}).start()

    def summed_q(n, h):
        wait_bytes(recv_q.at[n, h], qr_sem.at[n, h])
        total = product_block(1, h, me_t)
        for s in range(nt - 1):
            total = total + recv_q[n, h, s].astype(F32)
        return total

    def gather_q(n, h, v, piece):
        v[h][me_t] = piece.astype(BF16)
        for o in term_far:
            mine = v[h].at[me_t]
            pltpu.make_async_remote_copy(
                src_ref=mine, dst_ref=mine, send_sem=qas_sem.at[n, h], recv_sem=qar_sem.at[n, h],
                device_id={"term": term_peer(o)}).start()

    def gathered_q(n, h, v):
        wait_bytes(v[h].at[pl.ds(0, nt - 1)], qar_sem.at[n, h])

    def stats_start(n, row):
        st_term[n, me_t] = row

        @pl.loop(1, nt)
        def _(o):
            mine = st_term.at[n, me_t]
            pltpu.make_async_remote_copy(
                src_ref=mine, dst_ref=mine, send_sem=sts_sem.at[n], recv_sem=str_sem.at[n],
                device_id={"term": lax.rem(me_t + o, nt)}).start()

    def stats_turn(n):
        wait_bytes(st_term.at[n, pl.ds(0, nt - 1)], str_sem.at[n])
        total = st_term[n, 0]
        for s in range(1, nt):
            total = total + st_term[n, s]
        st_doc[n, me_d] = total
        for o in doc_far:
            mine = st_doc.at[n, me_d]
            pltpu.make_async_remote_copy(
                src_ref=mine, dst_ref=mine, send_sem=sds_sem.at[n], recv_sem=sdr_sem.at[n],
                device_id={"doc": doc_peer(o)}).start()

    def stats_end(n):
        wait_bytes(st_doc.at[n, pl.ds(0, nd - 1)], sdr_sem.at[n])
        total = st_doc[n, 0]
        for s in range(1, nd):
            total = total + st_doc[n, s]
        return total

    nothing = jnp.zeros((HALF, TILE), F32)

    for h in HALVES:
        product(0, vr0, h)
    pl.semaphore_wait(barrier, nd + nt - 2)
    for h in HALVES:
        scatter_g(0, h)

    @pl.loop(0, SLOTS // 32)
    def _(j):
        for u in range(32):
            tiles_t[j * 32 + u] = tiles[j * 32 + u].T

    p_sq = [nothing, nothing]
    for h in HALVES:
        scattered_g(0, h)
        for j in range(gp):
            total = summed_g(0, h, j)
            vp0[h][me_d * gp + j] = total.astype(BF16)
            s_held[h, j] = total
            p_sq[h] = p_sq[h] + total * total
        gather_g(0, h, vp0)

    for h in HALVES:
        gathered_g(0, h, vp0)
        product(1, vp0, h)
        scatter_q(0, h)
    row = jnp.zeros((1, TILE), F32)
    for h in HALVES:
        total = summed_q(0, h)
        gather_q(0, h, vq0, total)
        q_old[h] = total
        row = row + to_row(p_sq[h], h * HALF) + to_row(total * total + ridge[h] * p_sq[h], K + h * HALF)
    stats_start(0, row)

    for h in HALVES:
        gathered_q(0, h, vq0)
        product(0, vq0, h)
        scatter_g(1, h)
        if h == 0:
            stats_turn(0)
    stats = stats_end(0)
    grad_sq = [from_row(stats, h * HALF) for h in HALVES]
    step0 = [grad_sq[h] / from_row(stats, K + h * HALF) for h in HALVES]
    row = jnp.zeros((1, TILE), F32)
    for h in HALVES:
        scattered_g(1, h)
        g_sq = nothing
        for j in range(gp):
            p = s_held[h, j]
            x = step0[h] * p
            s = p - step0[h] * summed_g(1, h, j)
            g = s - ridge[h] * x
            vp1[h][me_d * gp + j] = g.astype(BF16)
            p_held[h, j] = p
            s_held[h, j] = s
            x_held[h, j] = x
            g_held[h, j] = g
            g_sq = g_sq + g * g
        gather_g(1, h, vp1)
        row = row + to_row(g_sq, h * HALF)
    stats_start(1, row)

    for h in HALVES:
        gathered_g(1, h, vp1)
        product(1, vp1, h)
        scatter_q(1, h)
        if h == 0:
            stats_turn(1)
    stats = stats_end(1)
    new_sq = [from_row(stats, h * HALF) for h in HALVES]
    beta = [new_sq[h] / grad_sq[h] for h in HALVES]
    row = jnp.zeros((1, TILE), F32)
    for h in HALVES:
        total = summed_q(1, h) + beta[h] * q_old[h]
        gather_q(1, h, vq1, total)
        p_sq = nothing
        for j in range(gp):
            p = g_held[h, j] + beta[h] * p_held[h, j]
            p_held[h, j] = p
            p_sq = p_sq + p * p
        row = row + to_row(total * total + ridge[h] * p_sq, h * HALF)
    stats_start(2, row)

    for h in HALVES:
        gathered_q(1, h, vq1)
        product(0, vq1, h)
        scatter_g(2, h)
        if h == 0:
            stats_turn(2)
    stats = stats_end(2)
    step1 = [new_sq[h] / from_row(stats, h * HALF) for h in HALVES]
    for h in HALVES:
        scattered_g(2, h)
        for j in range(gp):
            x = x_held[h, j] + step1[h] * p_held[h, j]
            s = s_held[h, j] - step1[h] * summed_g(2, h, j)
            vg[h][me_d * gp + j] = (s - ridge[h] * x).astype(BF16)
        gather_g(2, h, vg)
    for h in HALVES:
        rows = slice(h * HALF, (h + 1) * HALF)
        along0 = step0[h] + step1[h] * beta[h]
        for b in range(BLOCKS):
            lanes = slice(b * TILE, (b + 1) * TILE)
            x_out[rows, lanes] = along0 * vp0[h][b].astype(F32) + step1[h] * vp1[h][b].astype(F32)
            r_out[rows, lanes] = (targets[rows, lanes] - step0[h] * vq0[h][b].astype(F32)
                                  - step1[h] * vq1[h][b].astype(F32))
    for h in HALVES:
        gathered_g(2, h, vg)
        for b in range(BLOCKS):
            g_out[h * HALF:(h + 1) * HALF, b * TILE:(b + 1) * TILE] = vg[h][b].astype(F32)

    for n in range(3):
        for h in HALVES:
            wait_bytes(vg[h].at[pl.ds(0, (nd - 1) * gp)], gs_sem.at[n, h])
            wait_bytes(vg[h].at[pl.ds(0, (nd - 1) * gp)], pas_sem.at[n, h])
        wait_bytes(st_doc.at[n, pl.ds(0, nd - 1)], sds_sem.at[n])
        wait_bytes(st_term.at[n, pl.ds(0, nt - 1)], sts_sem.at[n])
    for n in range(2):
        for h in HALVES:
            wait_bytes(vq0[h].at[pl.ds(0, nt - 1)], qs_sem.at[n, h])
            wait_bytes(vq0[h].at[pl.ds(0, nt - 1)], qas_sem.at[n, h])


def store_kernel(x, r, g, x_out, r_out, g_out, sems):
    copies = [pltpu.make_async_copy(a, b, sems.at[i])
              for i, (a, b) in enumerate(((x, x_out), (r, r_out), (g, g_out)))]
    for copy in copies:
        copy.start()
    for copy in copies:
        copy.wait()


def on_device(nd, nt, tile_values, tile_row, tile_col, tile_count, targets, ridge_weight):
    gp = BLOCKS // nd
    hbm = pl.BlockSpec(memory_space=pl.ANY)
    vmem = pl.BlockSpec(memory_space=pltpu.VMEM)
    dma = pltpu.SemaphoreType.DMA
    out = jax.ShapeDtypeStruct((K, BLOCKS * TILE), F32)
    vector = pltpu.VMEM((BLOCKS + 1, HALF, TILE), BF16)
    piece = pltpu.VMEM((2, gp, HALF, TILE), F32)
    matrix = pltpu.VMEM((SLOTS, TILE, TILE), BF16)
    info = jnp.concatenate([
        tile_row.reshape(1, SLOTS).astype(F32),
        tile_col.reshape(1, SLOTS).astype(F32),
        jnp.broadcast_to(tile_count.astype(F32), (1, SLOTS)),
        jnp.pad(ridge_weight, (0, SLOTS - K)).reshape(1, SLOTS),
    ], axis=0)
    results = pl.pallas_call(
        functools.partial(cgls_kernel, nd, nt),
        out_shape=(out, out, out),
        in_specs=[hbm] * 3,
        out_specs=(vmem, vmem, vmem),
        scratch_shapes=[
            pltpu.VMEM((4, SLOTS), F32),
            pltpu.VMEM((8, PLACES), INT), pltpu.SMEM((8, PLACES), INT),
            pltpu.VMEM((K, BLOCKS * TILE), F32),
            matrix, matrix,
            pltpu.VMEM((2, PAIRS + 1, HALF, TILE), F32),
            [vector] * 12,
            pltpu.VMEM((3, 2, BLOCKS, HALF, TILE), BF16),
            pltpu.VMEM((3, 2, nd - 1, gp, HALF, TILE), BF16),
            pltpu.VMEM((2, 2, BLOCKS, HALF, TILE), BF16),
            pltpu.VMEM((2, 2, nt - 1, HALF, TILE), BF16),
            pltpu.VMEM((2, HALF, TILE), F32),
            piece, piece, piece, piece,
            pltpu.VMEM((3, nd, 1, TILE), F32),
            pltpu.VMEM((3, nt, 1, TILE), F32),
            dma(()), dma(()), dma(()),
            dma((LOADS,)), dma((3, 2)), dma((3, 2)), dma((2, 2)), dma((2, 2)),
            dma((3, 2)), dma((3, 2)), dma((2, 2)), dma((2, 2)),
            dma((3,)), dma((3,)), dma((3,)), dma((3,)),
        ],
        compiler_params=pltpu.CompilerParams(
            collective_id=0, has_side_effects=True, vmem_limit_bytes=48 * 1024 * 1024),
        name="cgls",
    )(info, targets, tile_values[0, 0])
    return pl.pallas_call(
        store_kernel,
        out_shape=(out, out, out),
        in_specs=[vmem] * 3,
        out_specs=(hbm, hbm, hbm),
        scratch_shapes=[dma((3,))],
        compiler_params=pltpu.CompilerParams(vmem_limit_bytes=2 * 1024 * 1024),
        name="store",
    )(*results)


def solution(mesh):
    nd, nt = mesh.shape["doc"], mesh.shape["term"]
    placed = (
        P("doc", "term", None, None, None),
        P("doc", "term", None),
        P("doc", "term", None),
        P("doc", "term"),
        P(None, "doc"),
        P(),
    )
    return jax.shard_map(
        functools.partial(on_device, nd, nt),
        mesh=mesh,
        in_specs=placed,
        out_specs=(P(None, "term"), P(None, "doc"), P(None, "term")),
        check_vma=False,
    )
```

```python
import functools

import jax
import jax.numpy as jnp
from jax import lax
from jax.experimental import pallas as pl
from jax.experimental.pallas import tpu as pltpu
from jax.sharding import PartitionSpec as P

TILE = 128
K = 32
BLOCKS = 32
SLOTS = 256
PAIRS = (SLOTS + BLOCKS) // 2
PLACES = 384
UNROLL = 72
LOADS = 8
HALF = K // 2
HALVES = range(2)
F32 = jnp.float32
BF16 = jnp.bfloat16
INT = jnp.int32


def iota(shape, dim):
    return lax.broadcasted_iota(INT, shape, dim)


def upright(row):
    square = (row.shape[1], row.shape[1])
    return jnp.sum(jnp.where(iota(square, 0) == iota(square, 1), row, 0.0), axis=1, keepdims=True)


def slot_table(dest, source, live, table):
    slot = iota((1, SLOTS), 1).astype(F32)
    block = iota((SLOTS, TILE), 1).astype(F32)
    place = iota((SLOTS, PLACES), 1).astype(F32)
    before = iota((TILE, TILE), 0) < iota((TILE, TILE), 1)
    dest = jnp.where(live, dest, float(BLOCKS))
    code = (dest * 64.0 + jnp.where(live, source, float(BLOCKS))) * SLOTS + slot
    code_up = upright(code)
    dest_up = upright(dest)
    here = dest_up == block
    size = jnp.sum(jnp.where(here, 1.0, 0.0), axis=0, keepdims=True).astype(INT)
    padded = jnp.bitwise_and(size + 1, -2)
    start = jnp.sum(jnp.where(before, upright(padded.astype(F32)), 0.0), axis=0, keepdims=True)
    within = jnp.sum(jnp.where(jnp.logical_and(code < code_up, dest == dest_up), 1.0, 0.0),
                     axis=1, keepdims=True)
    position = within + jnp.sum(jnp.where(here, start, 0.0), axis=1, keepdims=True)
    ordered = jnp.sum(jnp.where(position == place, code_up + 1.0, 0.0), axis=0, keepdims=True)
    ordered = ordered.astype(INT) - 1
    filled = ordered >= 0
    ordered = jnp.maximum(ordered, 0)
    dest_at = jnp.right_shift(ordered, 14)
    source_at = jnp.minimum(jnp.bitwise_and(jnp.right_shift(ordered, 8), 63), BLOCKS)
    same = jnp.where(dest_at == pltpu.roll(dest_at, 2, 1), 1, 0)
    last = jnp.right_shift(start.astype(INT) + padded, 1) - 1
    last = jnp.where(size > 0, jnp.clip(last, 0, PAIRS - 1), PAIRS)
    table[0:1, :] = jnp.bitwise_and(ordered, SLOTS - 1)
    table[1:2, :] = jnp.where(filled, source_at, BLOCKS)
    table[2:3, :] = same
    for part in range(PLACES // TILE):
        table[3:4, part * TILE:(part + 1) * TILE] = last


def to_row(values, base):
    total = jnp.sum(values, axis=1, keepdims=True)
    here = iota((HALF, TILE), 1) == iota((HALF, TILE), 0) + base
    return jnp.sum(jnp.where(here, total, 0.0), axis=0, keepdims=True)


def from_row(row, base):
    here = iota((HALF, TILE), 1) == iota((HALF, TILE), 0) + base
    return jnp.sum(jnp.where(here, row, 0.0), axis=1, keepdims=True)


def cgls_kernel(nd, nt, places, ridge_smem, targets_hbm, tiles_hbm,
                x_out, r_out, g_out,
                tables_v, tables, targets,
                tiles, tiles_t, prod, vectors,
                send_g, recv_g, send_q, recv_q, q_old, s_held, g_held, p_held, x_held,
                st_doc, st_term,
                table_sem, targets_sem,
                tile_sem, gs_sem, gr_sem, qs_sem, qr_sem, pas_sem, par_sem, qas_sem, qar_sem,
                sds_sem, sdr_sem, sts_sem, str_sem):
    me_d = lax.axis_index("doc")
    me_t = lax.axis_index("term")
    gp = BLOCKS // nd
    vr0, vp0, vp1, vg, vq0, vq1 = (vectors[2 * i:2 * i + 2] for i in range(6))

    barrier = pltpu.get_barrier_semaphore()

    load_targets = pltpu.make_async_copy(targets_hbm, targets, targets_sem)
    load_targets.start()
    part = SLOTS // LOADS
    load_tiles = [
        pltpu.make_async_copy(tiles_hbm.at[pl.ds(i * part, part)], tiles.at[pl.ds(i * part, part)],
                              tile_sem.at[i])
        for i in range(LOADS)
    ]
    for load in load_tiles:
        load.start()

    @pl.loop(1, nd)
    def _(o):
        pl.semaphore_signal(barrier, inc=1, device_id={"doc": lax.rem(me_d + o, nd)})

    @pl.loop(1, nt)
    def _(o):
        pl.semaphore_signal(barrier, inc=1, device_id={"term": lax.rem(me_t + o, nt)})

    zero = jnp.zeros((HALF, TILE), BF16)
    for h in HALVES:
        for v in (vr0, vp0, vp1, vq0, vq1):
            v[h][BLOCKS] = zero
        prod[h, PAIRS] = jnp.zeros((HALF, TILE), F32)

    def build_table(which):
        code = places[...]
        ends = (jnp.bitwise_and(code, BLOCKS - 1).astype(F32), jnp.right_shift(code, 5).astype(F32))
        slot_table(ends[which], ends[1 - which], code < BLOCKS * BLOCKS, tables_v[which])
        move = pltpu.make_async_copy(tables_v[which], tables[which], table_sem.at[which])
        move.start()
        return move

    move_table = build_table(0)
    ridge = []
    for h in HALVES:
        column = jnp.zeros((HALF, TILE), F32)
        for k in range(HALF):
            column = jnp.where(iota((HALF, TILE), 0) == k, ridge_smem[h * HALF + k], column)
        ridge.append(column)
    load_targets.wait()
    for b in range(BLOCKS):
        for h in HALVES:
            vr0[h][b] = targets[h * HALF:(h + 1) * HALF, b * TILE:(b + 1) * TILE].astype(BF16)
    move_table.wait()
    for load in load_tiles:
        load.wait()

    def product(which, v, h):
        matrix = tiles if which == 0 else tiles_t
        table = tables[which]

        def body(j, acc):
            for u in range(UNROLL):
                i = j * UNROLL + u
                left = jnp.concatenate([v[h][table[1, 2 * i + e]] for e in range(2)], axis=1)
                right = jnp.concatenate([matrix[table[0, 2 * i + e]] for e in range(2)], axis=0)
                acc = (acc * table[2, 2 * i].astype(F32)
                       + jnp.dot(left, right, preferred_element_type=F32))
                prod[h, i] = acc
            return acc

        lax.fori_loop(0, PAIRS // UNROLL, body, jnp.zeros((HALF, TILE), F32))

    def product_block(which, h, b):
        return prod[h, tables[which][3, b]]

    def wait_bytes(ref, sem):
        pltpu.make_async_copy(ref, ref, sem).wait()

    doc_far = sorted(range(1, nd), key=lambda o: -min(o, nd - o))
    ny, nx = nt // 8, 4
    term_far = sorted(
        ((y, x, c) for y in range(ny) for x in range(nx) for c in range(2) if (y, x, c) != (0, 0, 0)),
        key=lambda o: -(min(o[0], ny - o[0]) + min(o[1], nx - o[1])))

    def doc_peer(o):
        return lax.rem(me_d + o, nd)

    def term_peer(o):
        y = lax.rem(me_t // (2 * nx) + o[0], ny)
        x = lax.rem(lax.rem(me_t // 2, nx) + o[1], nx)
        c = lax.rem(me_t + o[2], 2)
        return (y * nx + x) * 2 + c

    def scatter_g(n, h):
        for b in range(BLOCKS):
            send_g[n, h, b] = product_block(0, h, b).astype(BF16)
        for i, o in enumerate(doc_far):
            to = doc_peer(o)
            pltpu.make_async_remote_copy(
                src_ref=send_g.at[n, h, pl.ds(to * gp, gp)], dst_ref=recv_g.at[n, h, i],
                send_sem=gs_sem.at[n, h], recv_sem=gr_sem.at[n, h], device_id={"doc": to}).start()

    def scattered_g(n, h):
        wait_bytes(recv_g.at[n, h], gr_sem.at[n, h])

    def summed_g(n, h, j):
        total = product_block(0, h, me_d * gp + j)
        for s in range(nd - 1):
            total = total + recv_g[n, h, s, j].astype(F32)
        return total

    def gather_g(n, h, v):
        for o in doc_far:
            mine = v[h].at[pl.ds(me_d * gp, gp)]
            pltpu.make_async_remote_copy(
                src_ref=mine, dst_ref=mine, send_sem=pas_sem.at[n, h], recv_sem=par_sem.at[n, h],
                device_id={"doc": doc_peer(o)}).start()

    def gathered_g(n, h, v):
        wait_bytes(v[h].at[pl.ds(0, (nd - 1) * gp)], par_sem.at[n, h])

    def scatter_q(n, h):
        for b in range(BLOCKS):
            send_q[n, h, b] = product_block(1, h, b).astype(BF16)
        for i, o in enumerate(term_far):
            to = term_peer(o)
            pltpu.make_async_remote_copy(
                src_ref=send_q.at[n, h, to], dst_ref=recv_q.at[n, h, i],
                send_sem=qs_sem.at[n, h], recv_sem=qr_sem.at[n, h], device_id={"term": to}).start()

    def summed_q(n, h):
        wait_bytes(recv_q.at[n, h], qr_sem.at[n, h])
        total = product_block(1, h, me_t)
        for s in range(nt - 1):
            total = total + recv_q[n, h, s].astype(F32)
        return total

    def gather_q(n, h, v, piece):
        v[h][me_t] = piece.astype(BF16)
        for o in term_far:
            mine = v[h].at[me_t]
            pltpu.make_async_remote_copy(
                src_ref=mine, dst_ref=mine, send_sem=qas_sem.at[n, h], recv_sem=qar_sem.at[n, h],
                device_id={"term": term_peer(o)}).start()

    def gathered_q(n, h, v):
        wait_bytes(v[h].at[pl.ds(0, nt - 1)], qar_sem.at[n, h])

    def stats_start(n, row):
        st_term[n, me_t] = row

        @pl.loop(1, nt)
        def _(o):
            mine = st_term.at[n, me_t]
            pltpu.make_async_remote_copy(
                src_ref=mine, dst_ref=mine, send_sem=sts_sem.at[n], recv_sem=str_sem.at[n],
                device_id={"term": lax.rem(me_t + o, nt)}).start()

    def stats_turn(n):
        wait_bytes(st_term.at[n, pl.ds(0, nt - 1)], str_sem.at[n])
        total = st_term[n, 0]
        for s in range(1, nt):
            total = total + st_term[n, s]
        st_doc[n, me_d] = total
        for o in doc_far:
            mine = st_doc.at[n, me_d]
            pltpu.make_async_remote_copy(
                src_ref=mine, dst_ref=mine, send_sem=sds_sem.at[n], recv_sem=sdr_sem.at[n],
                device_id={"doc": doc_peer(o)}).start()

    def stats_end(n):
        wait_bytes(st_doc.at[n, pl.ds(0, nd - 1)], sdr_sem.at[n])
        total = st_doc[n, 0]
        for s in range(1, nd):
            total = total + st_doc[n, s]
        return total

    nothing = jnp.zeros((HALF, TILE), F32)

    for h in HALVES:
        product(0, vr0, h)
        if h == 0:
            pl.semaphore_wait(barrier, nd + nt - 2)
        scatter_g(0, h)

    move_table = build_table(1)

    @pl.loop(0, SLOTS // 32)
    def _(j):
        for u in range(32):
            tiles_t[j * 32 + u] = tiles[j * 32 + u].T

    move_table.wait()

    p_sq = [nothing, nothing]
    for h in HALVES:
        scattered_g(0, h)
        for j in range(gp):
            total = summed_g(0, h, j)
            vp0[h][me_d * gp + j] = total.astype(BF16)
            s_held[h, j] = total
            p_sq[h] = p_sq[h] + total * total
        gather_g(0, h, vp0)

    for h in HALVES:
        gathered_g(0, h, vp0)
        product(1, vp0, h)
        scatter_q(0, h)
    row = jnp.zeros((1, TILE), F32)
    for h in HALVES:
        total = summed_q(0, h)
        gather_q(0, h, vq0, total)
        q_old[h] = total
        row = row + to_row(p_sq[h], h * HALF) + to_row(total * total + ridge[h] * p_sq[h], K + h * HALF)
    stats_start(0, row)

    for h in HALVES:
        gathered_q(0, h, vq0)
        product(0, vq0, h)
        scatter_g(1, h)
        if h == 0:
            stats_turn(0)
    stats = stats_end(0)
    grad_sq = [from_row(stats, h * HALF) for h in HALVES]
    step0 = [grad_sq[h] / from_row(stats, K + h * HALF) for h in HALVES]
    row = jnp.zeros((1, TILE), F32)
    for h in HALVES:
        scattered_g(1, h)
        g_sq = nothing
        for j in range(gp):
            p = s_held[h, j]
            x = step0[h] * p
            s = p - step0[h] * summed_g(1, h, j)
            g = s - ridge[h] * x
            vp1[h][me_d * gp + j] = g.astype(BF16)
            p_held[h, j] = p
            s_held[h, j] = s
            x_held[h, j] = x
            g_held[h, j] = g
            g_sq = g_sq + g * g
        gather_g(1, h, vp1)
        row = row + to_row(g_sq, h * HALF)
    stats_start(1, row)

    for h in HALVES:
        gathered_g(1, h, vp1)
        product(1, vp1, h)
        scatter_q(1, h)
        if h == 0:
            stats_turn(1)
    stats = stats_end(1)
    new_sq = [from_row(stats, h * HALF) for h in HALVES]
    beta = [new_sq[h] / grad_sq[h] for h in HALVES]
    row = jnp.zeros((1, TILE), F32)
    for h in HALVES:
        total = summed_q(1, h) + beta[h] * q_old[h]
        gather_q(1, h, vq1, total)
        p_sq = nothing
        for j in range(gp):
            p = g_held[h, j] + beta[h] * p_held[h, j]
            p_held[h, j] = p
            p_sq = p_sq + p * p
        row = row + to_row(total * total + ridge[h] * p_sq, h * HALF)
    stats_start(2, row)

    for h in HALVES:
        gathered_q(1, h, vq1)
        product(0, vq1, h)
        scatter_g(2, h)
        if h == 0:
            stats_turn(2)
    stats = stats_end(2)
    step1 = [new_sq[h] / from_row(stats, h * HALF) for h in HALVES]
    for h in HALVES:
        scattered_g(2, h)
        for j in range(gp):
            x = x_held[h, j] + step1[h] * p_held[h, j]
            s = s_held[h, j] - step1[h] * summed_g(2, h, j)
            vg[h][me_d * gp + j] = (s - ridge[h] * x).astype(BF16)
        gather_g(2, h, vg)
    for h in HALVES:
        rows = slice(h * HALF, (h + 1) * HALF)
        along0 = step0[h] + step1[h] * beta[h]
        for b in range(BLOCKS):
            lanes = slice(b * TILE, (b + 1) * TILE)
            x_out[rows, lanes] = along0 * vp0[h][b].astype(F32) + step1[h] * vp1[h][b].astype(F32)
            r_out[rows, lanes] = (targets[rows, lanes] - step0[h] * vq0[h][b].astype(F32)
                                  - step1[h] * vq1[h][b].astype(F32))
    for h in HALVES:
        gathered_g(2, h, vg)
        for b in range(BLOCKS):
            g_out[h * HALF:(h + 1) * HALF, b * TILE:(b + 1) * TILE] = vg[h][b].astype(F32)

    for n in range(3):
        for h in HALVES:
            wait_bytes(vg[h].at[pl.ds(0, (nd - 1) * gp)], gs_sem.at[n, h])
            wait_bytes(vg[h].at[pl.ds(0, (nd - 1) * gp)], pas_sem.at[n, h])
        wait_bytes(st_doc.at[n, pl.ds(0, nd - 1)], sds_sem.at[n])
        wait_bytes(st_term.at[n, pl.ds(0, nt - 1)], sts_sem.at[n])
    for n in range(2):
        for h in HALVES:
            wait_bytes(vq0[h].at[pl.ds(0, nt - 1)], qs_sem.at[n, h])
            wait_bytes(vq0[h].at[pl.ds(0, nt - 1)], qas_sem.at[n, h])


def store_kernel(x, r, g, x_out, r_out, g_out, sems):
    copies = [pltpu.make_async_copy(a, b, sems.at[i])
              for i, (a, b) in enumerate(((x, x_out), (r, r_out), (g, g_out)))]
    for copy in copies:
        copy.start()
    for copy in copies:
        copy.wait()


def on_device(nd, nt, tile_values, tile_row, tile_col, tile_count, targets, ridge_weight):
    gp = BLOCKS // nd
    hbm = pl.BlockSpec(memory_space=pl.ANY)
    vmem = pl.BlockSpec(memory_space=pltpu.VMEM)
    dma = pltpu.SemaphoreType.DMA
    out = jax.ShapeDtypeStruct((K, BLOCKS * TILE), F32)
    vector = pltpu.VMEM((BLOCKS + 1, HALF, TILE), BF16)
    piece = pltpu.VMEM((2, gp, HALF, TILE), F32)
    matrix = pltpu.VMEM((SLOTS, TILE, TILE), BF16)
    live = jnp.arange(SLOTS, dtype=INT).reshape(1, SLOTS) < tile_count
    places = jnp.where(live, tile_row[0] * BLOCKS + tile_col[0], BLOCKS * BLOCKS)
    results = pl.pallas_call(
        functools.partial(cgls_kernel, nd, nt),
        out_shape=(out, out, out),
        in_specs=[vmem, pl.BlockSpec(memory_space=pltpu.SMEM), hbm, hbm],
        out_specs=(vmem, vmem, vmem),
        scratch_shapes=[
            [pltpu.VMEM((4, PLACES), INT)] * 2, [pltpu.SMEM((4, PLACES), INT)] * 2,
            pltpu.VMEM((K, BLOCKS * TILE), F32),
            matrix, matrix,
            pltpu.VMEM((2, PAIRS + 1, HALF, TILE), F32),
            [vector] * 12,
            pltpu.VMEM((3, 2, BLOCKS, HALF, TILE), BF16),
            pltpu.VMEM((3, 2, nd - 1, gp, HALF, TILE), BF16),
            pltpu.VMEM((2, 2, BLOCKS, HALF, TILE), BF16),
            pltpu.VMEM((2, 2, nt - 1, HALF, TILE), BF16),
            pltpu.VMEM((2, HALF, TILE), F32),
            piece, piece, piece, piece,
            pltpu.VMEM((3, nd, 1, TILE), F32),
            pltpu.VMEM((3, nt, 1, TILE), F32),
            dma((2,)), dma(()),
            dma((LOADS,)), dma((3, 2)), dma((3, 2)), dma((2, 2)), dma((2, 2)),
            dma((3, 2)), dma((3, 2)), dma((2, 2)), dma((2, 2)),
            dma((3,)), dma((3,)), dma((3,)), dma((3,)),
        ],
        compiler_params=pltpu.CompilerParams(
            collective_id=0, has_side_effects=True, vmem_limit_bytes=52 * 1024 * 1024),
        name="cgls",
    )(places, ridge_weight, targets, tile_values[0, 0])
    return pl.pallas_call(
        store_kernel,
        out_shape=(out, out, out),
        in_specs=[vmem] * 3,
        out_specs=(hbm, hbm, hbm),
        scratch_shapes=[dma((3,))],
        compiler_params=pltpu.CompilerParams(vmem_limit_bytes=2 * 1024 * 1024),
        name="store",
    )(*results)


def solution(mesh):
    nd, nt = mesh.shape["doc"], mesh.shape["term"]
    placed = (
        P("doc", "term", None, None, None),
        P("doc", "term", None),
        P("doc", "term", None),
        P("doc", "term"),
        P(None, "doc"),
        P(),
    )
    return jax.shard_map(
        functools.partial(on_device, nd, nt),
        mesh=mesh,
        in_specs=placed,
        out_specs=(P(None, "term"), P(None, "doc"), P(None, "term")),
        check_vma=False,
    )
```

```python
import functools

import jax
import jax.numpy as jnp
from jax import lax
from jax.experimental import pallas as pl
from jax.experimental.pallas import tpu as pltpu
from jax.sharding import PartitionSpec as P

TILE = 128
K = 32
BLOCKS = 32
SLOTS = 256
PAIRS = (SLOTS + BLOCKS) // 2
PLACES = 384
UNROLL = 72
LOADS = 8
HALF = K // 2
HALVES = range(2)
F32 = jnp.float32
BF16 = jnp.bfloat16
INT = jnp.int32


def iota(shape, dim):
    return lax.broadcasted_iota(INT, shape, dim)


def upright(row):
    square = (row.shape[1], row.shape[1])
    return jnp.sum(jnp.where(iota(square, 0) == iota(square, 1), row, 0.0), axis=1, keepdims=True)


def slot_table(dest, source, live, table):
    slot = iota((1, SLOTS), 1).astype(F32)
    block = iota((SLOTS, TILE), 1).astype(F32)
    place = iota((SLOTS, PLACES), 1).astype(F32)
    before = iota((TILE, TILE), 0) < iota((TILE, TILE), 1)
    dest = jnp.where(live, dest, float(BLOCKS))
    code = (dest * 64.0 + jnp.where(live, source, float(BLOCKS))) * SLOTS + slot
    code_up = upright(code)
    dest_up = upright(dest)
    here = dest_up == block
    size = jnp.sum(jnp.where(here, 1.0, 0.0), axis=0, keepdims=True).astype(INT)
    padded = jnp.bitwise_and(size + 1, -2)
    start = jnp.sum(jnp.where(before, upright(padded.astype(F32)), 0.0), axis=0, keepdims=True)
    within = jnp.sum(jnp.where(jnp.logical_and(code < code_up, dest == dest_up), 1.0, 0.0),
                     axis=1, keepdims=True)
    position = within + jnp.sum(jnp.where(here, start, 0.0), axis=1, keepdims=True)
    ordered = jnp.sum(jnp.where(position == place, code_up + 1.0, 0.0), axis=0, keepdims=True)
    ordered = ordered.astype(INT) - 1
    filled = ordered >= 0
    ordered = jnp.maximum(ordered, 0)
    dest_at = jnp.right_shift(ordered, 14)
    source_at = jnp.minimum(jnp.bitwise_and(jnp.right_shift(ordered, 8), 63), BLOCKS)
    same = jnp.where(dest_at == pltpu.roll(dest_at, 2, 1), 1, 0)
    last = jnp.right_shift(start.astype(INT) + padded, 1) - 1
    last = jnp.where(size > 0, jnp.clip(last, 0, PAIRS - 1), PAIRS)
    table[0:1, :] = jnp.bitwise_and(ordered, SLOTS - 1)
    table[1:2, :] = jnp.where(filled, source_at, BLOCKS)
    table[2:3, :] = same
    for part in range(PLACES // TILE):
        table[3:4, part * TILE:(part + 1) * TILE] = last


def to_row(values, base):
    total = jnp.sum(values, axis=1, keepdims=True)
    here = iota((HALF, TILE), 1) == iota((HALF, TILE), 0) + base
    return jnp.sum(jnp.where(here, total, 0.0), axis=0, keepdims=True)


def from_row(row, base):
    here = iota((HALF, TILE), 1) == iota((HALF, TILE), 0) + base
    return jnp.sum(jnp.where(here, row, 0.0), axis=1, keepdims=True)


def cgls_kernel(nd, nt, places, ridge_smem, targets_hbm, tiles_hbm,
                x_out, r_out, g_out,
                tables_v, tables, targets,
                tiles, tiles_t, prod, vectors,
                send_g, recv_g, send_q, recv_q, q_old, s_held, g_held, p_held, x_held,
                st_doc, st_term,
                table_sem, targets_sem,
                tile_sem, gs_sem, gr_sem, qs_sem, qr_sem, pas_sem, par_sem, qas_sem, qar_sem,
                sds_sem, sdr_sem, sts_sem, str_sem):
    me_d = lax.axis_index("doc")
    me_t = lax.axis_index("term")
    gp = BLOCKS // nd
    vr0, vp0, vp1, vg, vq0, vq1 = (vectors[2 * i:2 * i + 2] for i in range(6))

    barrier = pltpu.get_barrier_semaphore()

    load_targets = pltpu.make_async_copy(targets_hbm, targets, targets_sem)
    load_targets.start()
    part = SLOTS // LOADS
    load_tiles = [
        pltpu.make_async_copy(tiles_hbm.at[pl.ds(i * part, part)], tiles.at[pl.ds(i * part, part)],
                              tile_sem.at[i])
        for i in range(LOADS)
    ]
    for load in load_tiles:
        load.start()

    @pl.loop(1, nd)
    def _(o):
        pl.semaphore_signal(barrier, inc=1, device_id={"doc": lax.rem(me_d + o, nd)})

    @pl.loop(1, nt)
    def _(o):
        pl.semaphore_signal(barrier, inc=1, device_id={"term": lax.rem(me_t + o, nt)})

    zero = jnp.zeros((HALF, TILE), BF16)
    for h in HALVES:
        for v in (vr0, vp0, vp1, vq0, vq1):
            v[h][BLOCKS] = zero
        prod[h, PAIRS] = jnp.zeros((HALF, TILE), F32)

    def build_table(which):
        code = places[...]
        ends = (jnp.bitwise_and(code, BLOCKS - 1).astype(F32), jnp.right_shift(code, 5).astype(F32))
        slot_table(ends[which], ends[1 - which], code < BLOCKS * BLOCKS, tables_v[which])
        move = pltpu.make_async_copy(tables_v[which], tables[which], table_sem.at[which])
        move.start()
        return move

    move_table = build_table(0)
    ridge = []
    for h in HALVES:
        column = jnp.zeros((HALF, TILE), F32)
        for k in range(HALF):
            column = jnp.where(iota((HALF, TILE), 0) == k, ridge_smem[h * HALF + k], column)
        ridge.append(column)
    load_targets.wait()
    for b in range(BLOCKS):
        for h in HALVES:
            vr0[h][b] = targets[h * HALF:(h + 1) * HALF, b * TILE:(b + 1) * TILE].astype(BF16)
    move_table.wait()
    for load in load_tiles:
        load.wait()

    def product(which, v, h):
        matrix = tiles if which == 0 else tiles_t
        table = tables[which]

        def body(j, acc):
            for u in range(UNROLL):
                i = j * UNROLL + u
                left = jnp.concatenate([v[h][table[1, 2 * i + e]] for e in range(2)], axis=1)
                right = jnp.concatenate([matrix[table[0, 2 * i + e]] for e in range(2)], axis=0)
                acc = (acc * table[2, 2 * i].astype(F32)
                       + jnp.dot(left, right, preferred_element_type=F32))
                prod[h, i] = acc
            return acc

        lax.fori_loop(0, PAIRS // UNROLL, body, jnp.zeros((HALF, TILE), F32))

    def product_block(which, h, b):
        return prod[h, tables[which][3, b]]

    def wait_bytes(ref, sem):
        pltpu.make_async_copy(ref, ref, sem).wait()

    doc_far = sorted(range(1, nd), key=lambda o: -min(o, nd - o))
    ny, nx = nt // 8, 4
    term_far = sorted(
        ((y, x, c) for y in range(ny) for x in range(nx) for c in range(2) if (y, x, c) != (0, 0, 0)),
        key=lambda o: -(min(o[0], ny - o[0]) + min(o[1], nx - o[1])))

    def doc_peer(o):
        return lax.rem(me_d + o, nd)

    def term_peer(o):
        y = lax.rem(me_t // (2 * nx) + o[0], ny)
        x = lax.rem(lax.rem(me_t // 2, nx) + o[1], nx)
        c = lax.rem(me_t + o[2], 2)
        return (y * nx + x) * 2 + c

    def scatter_g(n, h):
        for i, o in enumerate(doc_far):
            to = doc_peer(o)
            for j in range(gp):
                send_g[n, h, to * gp + j] = product_block(0, h, to * gp + j).astype(BF16)
            pltpu.make_async_remote_copy(
                src_ref=send_g.at[n, h, pl.ds(to * gp, gp)], dst_ref=recv_g.at[n, h, i],
                send_sem=gs_sem.at[n, h], recv_sem=gr_sem.at[n, h], device_id={"doc": to}).start()

    def scattered_g(n, h):
        wait_bytes(recv_g.at[n, h], gr_sem.at[n, h])

    def summed_g(n, h, j):
        total = product_block(0, h, me_d * gp + j)
        for s in range(nd - 1):
            total = total + recv_g[n, h, s, j].astype(F32)
        return total

    def gather_g(n, h, v):
        for o in doc_far:
            mine = v[h].at[pl.ds(me_d * gp, gp)]
            pltpu.make_async_remote_copy(
                src_ref=mine, dst_ref=mine, send_sem=pas_sem.at[n, h], recv_sem=par_sem.at[n, h],
                device_id={"doc": doc_peer(o)}).start()

    def gathered_g(n, h, v):
        wait_bytes(v[h].at[pl.ds(0, (nd - 1) * gp)], par_sem.at[n, h])

    def scatter_q(n, h):
        for i, o in enumerate(term_far):
            to = term_peer(o)
            send_q[n, h, to] = product_block(1, h, to).astype(BF16)
            pltpu.make_async_remote_copy(
                src_ref=send_q.at[n, h, to], dst_ref=recv_q.at[n, h, i],
                send_sem=qs_sem.at[n, h], recv_sem=qr_sem.at[n, h], device_id={"term": to}).start()

    def summed_q(n, h):
        wait_bytes(recv_q.at[n, h], qr_sem.at[n, h])
        total = product_block(1, h, me_t)
        for s in range(nt - 1):
            total = total + recv_q[n, h, s].astype(F32)
        return total

    def gather_q(n, h, v, piece):
        v[h][me_t] = piece.astype(BF16)
        for o in term_far:
            mine = v[h].at[me_t]
            pltpu.make_async_remote_copy(
                src_ref=mine, dst_ref=mine, send_sem=qas_sem.at[n, h], recv_sem=qar_sem.at[n, h],
                device_id={"term": term_peer(o)}).start()

    def gathered_q(n, h, v):
        wait_bytes(v[h].at[pl.ds(0, nt - 1)], qar_sem.at[n, h])

    def stats_start(n, row):
        st_term[n, me_t] = row

        @pl.loop(1, nt)
        def _(o):
            mine = st_term.at[n, me_t]
            pltpu.make_async_remote_copy(
                src_ref=mine, dst_ref=mine, send_sem=sts_sem.at[n], recv_sem=str_sem.at[n],
                device_id={"term": lax.rem(me_t + o, nt)}).start()

    def stats_turn(n):
        wait_bytes(st_term.at[n, pl.ds(0, nt - 1)], str_sem.at[n])
        total = st_term[n, 0]
        for s in range(1, nt):
            total = total + st_term[n, s]
        st_doc[n, me_d] = total
        for o in doc_far:
            mine = st_doc.at[n, me_d]
            pltpu.make_async_remote_copy(
                src_ref=mine, dst_ref=mine, send_sem=sds_sem.at[n], recv_sem=sdr_sem.at[n],
                device_id={"doc": doc_peer(o)}).start()

    def stats_end(n):
        wait_bytes(st_doc.at[n, pl.ds(0, nd - 1)], sdr_sem.at[n])
        total = st_doc[n, 0]
        for s in range(1, nd):
            total = total + st_doc[n, s]
        return total

    nothing = jnp.zeros((HALF, TILE), F32)

    for h in HALVES:
        product(0, vr0, h)
        if h == 0:
            pl.semaphore_wait(barrier, nd + nt - 2)
        scatter_g(0, h)

    def transpose(first, count):
        @pl.loop(first // 32, (first + count) // 32)
        def _(j):
            for u in range(32):
                tiles_t[j * 32 + u] = tiles[j * 32 + u].T

    move_table = build_table(1)
    transpose(0, SLOTS // 4)
    move_table.wait()
    p_sq = [nothing, nothing]
    for h in HALVES:
        scattered_g(0, h)
        for j in range(gp):
            total = summed_g(0, h, j)
            vp0[h][me_d * gp + j] = total.astype(BF16)
            s_held[h, j] = total
            p_sq[h] = p_sq[h] + total * total
        gather_g(0, h, vp0)
    transpose(SLOTS // 4, 3 * SLOTS // 4)

    for h in HALVES:
        gathered_g(0, h, vp0)
        product(1, vp0, h)
        scatter_q(0, h)
    row = jnp.zeros((1, TILE), F32)
    for h in HALVES:
        total = summed_q(0, h)
        gather_q(0, h, vq0, total)
        q_old[h] = total
        row = row + to_row(p_sq[h], h * HALF) + to_row(total * total + ridge[h] * p_sq[h], K + h * HALF)
    stats_start(0, row)

    for h in HALVES:
        gathered_q(0, h, vq0)
        product(0, vq0, h)
        scatter_g(1, h)
        if h == 0:
            stats_turn(0)
    stats = stats_end(0)
    grad_sq = [from_row(stats, h * HALF) for h in HALVES]
    step0 = [grad_sq[h] / from_row(stats, K + h * HALF) for h in HALVES]
    row = jnp.zeros((1, TILE), F32)
    for h in HALVES:
        scattered_g(1, h)
        g_sq = nothing
        for j in range(gp):
            p = s_held[h, j]
            x = step0[h] * p
            s = p - step0[h] * summed_g(1, h, j)
            g = s - ridge[h] * x
            vp1[h][me_d * gp + j] = g.astype(BF16)
            p_held[h, j] = p
            s_held[h, j] = s
            x_held[h, j] = x
            g_held[h, j] = g
            g_sq = g_sq + g * g
        gather_g(1, h, vp1)
        row = row + to_row(g_sq, h * HALF)
    stats_start(1, row)

    for h in HALVES:
        gathered_g(1, h, vp1)
        product(1, vp1, h)
        scatter_q(1, h)
        if h == 0:
            stats_turn(1)
    stats = stats_end(1)
    new_sq = [from_row(stats, h * HALF) for h in HALVES]
    beta = [new_sq[h] / grad_sq[h] for h in HALVES]
    row = jnp.zeros((1, TILE), F32)
    for h in HALVES:
        total = summed_q(1, h) + beta[h] * q_old[h]
        gather_q(1, h, vq1, total)
        p_sq = nothing
        for j in range(gp):
            p = g_held[h, j] + beta[h] * p_held[h, j]
            p_held[h, j] = p
            p_sq = p_sq + p * p
        row = row + to_row(total * total + ridge[h] * p_sq, h * HALF)
    stats_start(2, row)

    for h in HALVES:
        gathered_q(1, h, vq1)
        product(0, vq1, h)
        scatter_g(2, h)
        if h == 0:
            stats_turn(2)
    stats = stats_end(2)
    step1 = [new_sq[h] / from_row(stats, h * HALF) for h in HALVES]
    for h in HALVES:
        scattered_g(2, h)
        for j in range(gp):
            x = x_held[h, j] + step1[h] * p_held[h, j]
            s = s_held[h, j] - step1[h] * summed_g(2, h, j)
            vg[h][me_d * gp + j] = (s - ridge[h] * x).astype(BF16)
        gather_g(2, h, vg)
    for h in HALVES:
        rows = slice(h * HALF, (h + 1) * HALF)
        along0 = step0[h] + step1[h] * beta[h]
        for b in range(BLOCKS):
            lanes = slice(b * TILE, (b + 1) * TILE)
            x_out[rows, lanes] = along0 * vp0[h][b].astype(F32) + step1[h] * vp1[h][b].astype(F32)
            r_out[rows, lanes] = (targets[rows, lanes] - step0[h] * vq0[h][b].astype(F32)
                                  - step1[h] * vq1[h][b].astype(F32))
    for h in HALVES:
        gathered_g(2, h, vg)
        for b in range(BLOCKS):
            g_out[h * HALF:(h + 1) * HALF, b * TILE:(b + 1) * TILE] = vg[h][b].astype(F32)

    for n in range(3):
        for h in HALVES:
            wait_bytes(vg[h].at[pl.ds(0, (nd - 1) * gp)], gs_sem.at[n, h])
            wait_bytes(vg[h].at[pl.ds(0, (nd - 1) * gp)], pas_sem.at[n, h])
        wait_bytes(st_doc.at[n, pl.ds(0, nd - 1)], sds_sem.at[n])
        wait_bytes(st_term.at[n, pl.ds(0, nt - 1)], sts_sem.at[n])
    for n in range(2):
        for h in HALVES:
            wait_bytes(vq0[h].at[pl.ds(0, nt - 1)], qs_sem.at[n, h])
            wait_bytes(vq0[h].at[pl.ds(0, nt - 1)], qas_sem.at[n, h])


def store_kernel(x, r, g, x_out, r_out, g_out, sems):
    copies = [pltpu.make_async_copy(a, b, sems.at[i])
              for i, (a, b) in enumerate(((x, x_out), (r, r_out), (g, g_out)))]
    for copy in copies:
        copy.start()
    for copy in copies:
        copy.wait()


def on_device(nd, nt, tile_values, tile_row, tile_col, tile_count, targets, ridge_weight):
    gp = BLOCKS // nd
    hbm = pl.BlockSpec(memory_space=pl.ANY)
    vmem = pl.BlockSpec(memory_space=pltpu.VMEM)
    dma = pltpu.SemaphoreType.DMA
    out = jax.ShapeDtypeStruct((K, BLOCKS * TILE), F32)
    vector = pltpu.VMEM((BLOCKS + 1, HALF, TILE), BF16)
    piece = pltpu.VMEM((2, gp, HALF, TILE), F32)
    matrix = pltpu.VMEM((SLOTS, TILE, TILE), BF16)
    live = jnp.arange(SLOTS, dtype=INT).reshape(1, SLOTS) < tile_count
    places = jnp.where(live, tile_row[0] * BLOCKS + tile_col[0], BLOCKS * BLOCKS)
    results = pl.pallas_call(
        functools.partial(cgls_kernel, nd, nt),
        out_shape=(out, out, out),
        in_specs=[vmem, pl.BlockSpec(memory_space=pltpu.SMEM), hbm, hbm],
        out_specs=(vmem, vmem, vmem),
        scratch_shapes=[
            [pltpu.VMEM((4, PLACES), INT)] * 2, [pltpu.SMEM((4, PLACES), INT)] * 2,
            pltpu.VMEM((K, BLOCKS * TILE), F32),
            matrix, matrix,
            pltpu.VMEM((2, PAIRS + 1, HALF, TILE), F32),
            [vector] * 12,
            pltpu.VMEM((3, 2, BLOCKS, HALF, TILE), BF16),
            pltpu.VMEM((3, 2, nd - 1, gp, HALF, TILE), BF16),
            pltpu.VMEM((2, 2, BLOCKS, HALF, TILE), BF16),
            pltpu.VMEM((2, 2, nt - 1, HALF, TILE), BF16),
            pltpu.VMEM((2, HALF, TILE), F32),
            piece, piece, piece, piece,
            pltpu.VMEM((3, nd, 1, TILE), F32),
            pltpu.VMEM((3, nt, 1, TILE), F32),
            dma((2,)), dma(()),
            dma((LOADS,)), dma((3, 2)), dma((3, 2)), dma((2, 2)), dma((2, 2)),
            dma((3, 2)), dma((3, 2)), dma((2, 2)), dma((2, 2)),
            dma((3,)), dma((3,)), dma((3,)), dma((3,)),
        ],
        compiler_params=pltpu.CompilerParams(
            collective_id=0, has_side_effects=True, vmem_limit_bytes=52 * 1024 * 1024),
        name="cgls",
    )(places, ridge_weight, targets, tile_values[0, 0])
    return pl.pallas_call(
        store_kernel,
        out_shape=(out, out, out),
        in_specs=[vmem] * 3,
        out_specs=(hbm, hbm, hbm),
        scratch_shapes=[dma((3,))],
        compiler_params=pltpu.CompilerParams(vmem_limit_bytes=2 * 1024 * 1024),
        name="store",
    )(*results)


def solution(mesh):
    nd, nt = mesh.shape["doc"], mesh.shape["term"]
    placed = (
        P("doc", "term", None, None, None),
        P("doc", "term", None),
        P("doc", "term", None),
        P("doc", "term"),
        P(None, "doc"),
        P(),
    )
    return jax.shard_map(
        functools.partial(on_device, nd, nt),
        mesh=mesh,
        in_specs=placed,
        out_specs=(P(None, "term"), P(None, "doc"), P(None, "term")),
        check_vma=False,
    )
```
